768 devices in a mesh: seq: 32 (over y, x), pipe: 2 (over core), head: 12 (over z).
Axes of the slice: x: 4, y: 8, z: 12, core: 2. Of those that a mesh axis runs over, the one named last changes fastest.
Arguments:
- qk_rows: bfloat16 [2, 8192, 12, 128], P('pipe', 'seq', 'head'), may hold values from -6 to 6
- vu_rows: bfloat16 [2, 8192, 12, 128], P('pipe', 'seq', 'head'), may hold values from -6 to 6
- grad_next: bfloat16 [2, 8192, 12, 64], P('pipe', 'seq', 'head'), may hold values from -6 to 6
- layer_gain: float32 [12, 64], P('head'), may hold values from 0.1 to 1.9
- user_lengths: int32 [2, 4], P('pipe'), may hold values from 1 to 4096, 8192 in all within a row
Outputs:
- grad_qk: bfloat16 [2, 8192, 12, 128], P('pipe', 'seq', 'head')
- grad_vu: bfloat16 [2, 8192, 12, 128], P('pipe', 'seq', 'head')
The draws below stay inside these ranges and needn't reach their ends.
Inputs may be any that keep to these rules, and one draw needn't show every extreme that they name: `user_lengths`: each row of lengths lays its users' histories end to end over all 8192 rows; no history is longer than 4096 rows, and some history is exactly 4096 rows long.
All inputs are finite; a program needn't handle non-finite values.
Results may differ from the reference program's by a relative error of at most 0.006.
Values may be sent and summed in bfloat16 or wider, within the bound.
A program may use at most 32 MiB of HBM per device.

```python
import math
import jax
import jax.numpy as jnp
import numpy as np
from jax import lax

DH = 64
HEADS = 12
BLOCK = 256
ROWS = 8192
MICRO = 2
MOST = 4096
USERS = 4


def steps_of(rng, extent, pieces, low, high):
    gain, own = 1.0, jax.random.fold_in(rng, 6)
    for position, blocks in pieces:
        heights = jnp.exp(jax.random.uniform(jax.random.fold_in(own, position), (blocks,), jnp.float32, low / len(pieces), high / len(pieces)))
        gain = gain * jnp.repeat(heights, extent[position] // blocks).reshape([-1 if axis == position else 1 for axis in range(len(extent))])
    return gain


def length_profile(amount, total, limit, lean):
    weights = [(1 << 20) // math.isqrt(standing ** lean) + 1 for standing in range(2, amount + 1)]
    rest, counts = total - limit - (amount - 1), [1] * (amount - 1)
    while rest > 0:
        movable = [i for i in range(amount - 1) if counts[i] < limit]
        mass, left = sum([weights[i] for i in movable]), rest
        for i in movable:
            addition = min(limit - counts[i], max(1, left * weights[i] // mass), rest)
            counts[i] = counts[i] + addition
            rest = rest - addition
    return np.array([limit] + counts)


def ragged_sizes(stream_key, number_of, total, bound, skew):
    if number_of == 2:
        one = jax.random.randint(stream_key, (), max(1, total - bound), min(bound, total - 1) + 1)
        return jnp.stack([one, total - one])
    lengths = jnp.asarray(length_profile(number_of, total, bound, skew), jnp.int32)
    pairs = (number_of - 1) // 2
    donor, taker = lengths[1:1 + 2 * pairs:2], lengths[2:2 + 2 * pairs:2]
    margin = jnp.minimum(donor - 1, bound - taker)
    shifted = jax.random.randint(jax.random.fold_in(stream_key, 1), (pairs,), 0, 1 << 20) % (margin + 1)
    lengths = lengths.at[1:1 + 2 * pairs:2].set(donor - shifted).at[2:2 + 2 * pairs:2].set(taker + shifted)
    return lengths[jax.random.permutation(jax.random.fold_in(stream_key, 2), number_of)]


def bell_draw(rng, dims, deviation, most, pieces=(), held_as=jnp.bfloat16):
    level = steps_of(rng, dims, pieces, -0.22, 0.18) if pieces else 1.0
    entries = jax.random.normal(rng, dims, jnp.float32) * deviation * level
    return jnp.minimum(jnp.maximum(entries, -most), most).astype(held_as)


def setup_inputs(seed: int = 0) -> dict:
    key_of = jax.random.split(jax.random.key(seed), 6)
    qk_rows = bell_draw(key_of[0], (MICRO, ROWS, HEADS, 2 * DH), 1.0, 6.0, ((0, 2), (1, 32), (2, 12)))
    vu_rows = bell_draw(key_of[1], (MICRO, ROWS, HEADS, 2 * DH), 1.0, 6.0, ((0, 2), (1, 32), (2, 12)))
    grad_next = bell_draw(key_of[2], (MICRO, ROWS, HEADS, DH), 1.0, 6.0, ((0, 2), (1, 32), (2, 12)))
    layer_gain = jnp.clip(1.0 + 0.18 * jax.random.normal(key_of[3], (HEADS, DH), jnp.float32), 0.1, 1.9)
    user_lengths = jax.vmap(lambda own: ragged_sizes(own, USERS, ROWS, MOST, 2))(jax.random.split(key_of[4], MICRO)).reshape((MICRO, USERS)).astype(jnp.int32)
    return dict(qk_rows=qk_rows, vu_rows=vu_rows, grad_next=grad_next, layer_gain=layer_gain, user_lengths=user_lengths)


weight_scale = 1.0 / 256.0

def row_segments(positions, user_ends):
    segment = lax.optimization_barrier(jnp.sum((positions[:, None] >= user_ends[None, :]).astype(jnp.int32), axis=1))
    return jnp.where(positions < 0, -1, segment).astype(jnp.int32)

def reference(qk_rows, vu_rows, grad_next, layer_gain, user_lengths):
    score_scale = DH ** (-0.5)
    window = MOST + BLOCK
    blocks = ROWS // BLOCK
    features = HEADS * DH
    grads_all = jnp.roll(grad_next, 1, axis=0)
    qk_out = []
    vu_out = []
    for micro_index in range(MICRO):
        queries = qk_rows[micro_index, :, :, :DH]
        keys = qk_rows[micro_index, :, :, DH:]
        values = vu_rows[micro_index, :, :, :DH]
        gates_u = vu_rows[micro_index, :, :, DH:]
        user_ends = jnp.cumsum(user_lengths[micro_index]).astype(jnp.int32)
        positions = jnp.arange(ROWS, dtype=jnp.int32)
        segment = row_segments(positions, user_ends)
        key_pad = jnp.concatenate([jnp.zeros((MOST, HEADS, DH), keys.dtype), keys], axis=0)
        value_pad = jnp.concatenate([jnp.zeros((MOST, HEADS, DH), values.dtype), values], axis=0)
        seg_pad = jnp.concatenate([jnp.full((MOST,), -1, jnp.int32), segment])

        def window_of(block_index):
            block_start = (block_index * BLOCK).astype(jnp.int32)
            q_block = lax.dynamic_slice_in_dim(queries, block_start, BLOCK, 0)
            k_window = lax.dynamic_slice_in_dim(key_pad, block_start, window, 0)
            v_window = lax.dynamic_slice_in_dim(value_pad, block_start, window, 0)
            key_seg = lax.dynamic_slice_in_dim(seg_pad, block_start, window, 0)
            query_seg = lax.dynamic_slice_in_dim(segment, block_start, BLOCK, 0)
            query_pos = block_start + jnp.arange(BLOCK, dtype=jnp.int32)
            key_pos = block_start - MOST + jnp.arange(window, dtype=jnp.int32)
            live_mask = (query_seg[:, None] == key_seg[None, :]) & (key_pos[None, :] <= query_pos[:, None])
            scores = jnp.einsum('qhd,khd->hqk', q_block.astype(jnp.float32), k_window.astype(jnp.float32)) * score_scale
            return (block_start, q_block, k_window, v_window, live_mask, scores)

        def attend(block_index):
            found = window_of(block_index)
            v_window, live_mask, scores = (found[3], found[4], found[5])
            weights = jnp.where(live_mask[None], scores * jax.nn.sigmoid(scores) * weight_scale, 0.0).astype(jnp.bfloat16)
            weights = lax.optimization_barrier(weights)
            return jnp.einsum('hqk,khd->qhd', weights.astype(jnp.float32), v_window.astype(jnp.float32))
        attended = lax.map(attend, jnp.arange(blocks, dtype=jnp.int32)).reshape(ROWS, HEADS, DH)
        sum_one = lax.optimization_barrier(jnp.sum(attended, axis=(1, 2)))
        sum_two = lax.optimization_barrier(jnp.sum(attended * attended, axis=(1, 2)))
        row_mean = sum_one / features
        row_var = jnp.maximum(sum_two / features - row_mean * row_mean, 0.0)
        row_sigma = jnp.sqrt(row_var + 1e-05)
        normed = (attended - row_mean[:, None, None]) / row_sigma[:, None, None]
        grad_f = grads_all[micro_index].astype(jnp.float32)
        gain_f = layer_gain[None].astype(jnp.float32)
        d_gate = (grad_f * normed * gain_f).astype(jnp.bfloat16)
        grad_norm = grad_f * gates_u.astype(jnp.float32) * gain_f
        tot_one = lax.optimization_barrier(jnp.sum(grad_norm, axis=(1, 2)))
        tot_two = lax.optimization_barrier(jnp.sum(grad_norm * normed, axis=(1, 2)))
        grad_attn = ((grad_norm - (tot_one / features)[:, None, None] - normed * (tot_two / features)[:, None, None]) / row_sigma[:, None, None]).astype(jnp.bfloat16)
        grad_attn = lax.optimization_barrier(grad_attn)

        def back_step(carry, block_index):
            key_acc, value_acc = carry
            block_start, q_block, k_window, v_window, live_mask, scores = window_of(block_index)
            grad_block = lax.dynamic_slice_in_dim(grad_attn, block_start, BLOCK, 0).astype(jnp.float32)
            sig_gate = jax.nn.sigmoid(scores)
            weights = jnp.where(live_mask[None], scores * sig_gate * weight_scale, 0.0).astype(jnp.bfloat16)
            weights = lax.optimization_barrier(weights)
            d_values = jnp.einsum('hqk,qhd->khd', weights.astype(jnp.float32), grad_block)
            d_weights = jnp.einsum('qhd,khd->hqk', grad_block, v_window.astype(jnp.float32))
            d_scores = jnp.where(live_mask[None], d_weights * sig_gate * (1.0 + scores * (1.0 - sig_gate)) * (weight_scale * score_scale), 0.0).astype(jnp.bfloat16)
            d_scores = lax.optimization_barrier(d_scores)
            d_queries = jnp.einsum('hqk,khd->qhd', d_scores.astype(jnp.float32), k_window.astype(jnp.float32))
            d_keys = jnp.einsum('hqk,qhd->khd', d_scores.astype(jnp.float32), q_block.astype(jnp.float32))
            key_acc = lax.dynamic_update_slice_in_dim(key_acc, lax.dynamic_slice_in_dim(key_acc, block_start, window, 0) + d_keys, block_start, 0)
            value_acc = lax.dynamic_update_slice_in_dim(value_acc, lax.dynamic_slice_in_dim(value_acc, block_start, window, 0) + d_values, block_start, 0)
            return ((key_acc, value_acc), d_queries)
        zeros_acc = jnp.zeros((MOST + ROWS, HEADS, DH), jnp.float32)
        (key_acc, value_acc), d_queries = lax.scan(back_step, (zeros_acc, zeros_acc), jnp.arange(blocks, dtype=jnp.int32))
        d_queries = d_queries.reshape(ROWS, HEADS, DH)
        qk_out.append(jnp.concatenate([d_queries, key_acc[MOST:]], axis=2).astype(jnp.bfloat16))
        vu_out.append(jnp.concatenate([value_acc[MOST:].astype(jnp.bfloat16), d_gate], axis=2))
    return (jnp.stack(qk_out), jnp.stack(vu_out))
```

```python
import jax
import jax.numpy as jnp
from jax import lax
from jax.experimental import pallas as pl
from jax.experimental.pallas import tpu as pltpu
from jax.sharding import PartitionSpec as P

MESH = pl.DeviceIdType.MESH
F32 = jnp.float32
BF16 = jnp.bfloat16
COLS = 4
REACH = 4
HALF = 64


def kernel(
    qk_ref, vu_ref, gr_ref, gain_ref, len_ref,
    oqk_ref, ovu_ref,
    kv, kvt, pt, gf, stat, grx, psend, precv, relay, ych, ysend, own,
    g_sem, yf_send, yf_recv, xf_send, xf_recv, z_send, z_recv, xb_send, xb_recv, yb_send, yb_recv,
):
    rows = qk_ref.shape[0]
    seqs = lax.axis_size("seq")
    heads = lax.axis_size("head")
    s, z, core = lax.axis_index("seq"), lax.axis_index("head"), lax.axis_index("pipe")
    x, y = s % COLS, s // COLS
    tall = seqs // COLS

    def col(j):
        return (x + j) % COLS

    east = {"seq": y * COLS + col(1)}
    west = {"seq": y * COLS + col(COLS - 1)}
    north = {"seq": ((y + 1) % tall) * COLS + x}
    south = {"seq": ((y + tall - 1) % tall) * COLS + x}
    partner = {"pipe": 1 - core}

    def remote(src, dst, send, recv, to):
        return pltpu.make_async_remote_copy(
            src_ref=src, dst_ref=dst, send_sem=send, recv_sem=recv, device_id=to, device_id_type=MESH
        )

    barrier = pltpu.get_barrier_semaphore()
    for to in (east, west, north, south, partner):
        pl.semaphore_signal(barrier, inc=1, device_id=to, device_id_type=MESH)

    def greet(k, carry):
        pl.semaphore_signal(barrier, inc=1, device_id={"head": (z + k) % heads}, device_id_type=MESH)
        return carry

    lax.fori_loop(1, heads, greet, 0)

    qk = qk_ref[...]
    vu = vu_ref[...]
    kv[0, x] = jnp.concatenate([qk[:, HALF:], vu[:, :HALF]], axis=1)
    lane = lax.broadcasted_iota(jnp.int32, (rows, 2 * HALF), 1)
    sub = lax.broadcasted_iota(jnp.int32, (2 * HALF, rows), 0)
    qk_t = qk.astype(F32).T
    qz = jnp.where(sub < HALF, qk_t * (0.5 * HALF ** -0.5), 0.0).astype(BF16)
    position = s * rows + lax.broadcasted_iota(jnp.int32, (1, rows), 1)
    start = jnp.zeros((1, rows), jnp.int32)
    end = 0
    for user in range(len_ref.shape[1]):
        end = end + len_ref[0, user]
        start = jnp.where(position >= end, end, start)
    key_row = lax.broadcasted_iota(jnp.int32, (rows, rows), 0)

    pl.semaphore_wait(barrier, heads - 1 + 5)

    grads = remote(gr_ref, grx, g_sem.at[0], g_sem.at[1], partner)

    def y_fwd(r):
        return remote(kv.at[r, x], kv.at[r + 1, x], yf_send.at[r], yf_recv.at[r], north)

    def x_fwd(r, way):
        c, to, part = (
            (x, east, slice(None)),
            (x, west, slice(None)),
            (col(COLS - 1), east, slice(0, rows // 2)),
            (col(1), west, slice(rows // 2, rows)),
        )[way]
        if way < 2:
            ref = kv.at[r, c]
        else:
            ref = kv.at[r, c, pl.ds(part.start, rows // 2)]
        return remote(ref, ref, xf_send.at[r, way], xf_recv.at[r, way], to)

    def x_fwd_here(r, way):
        c = (col(COLS - 1), col(1), col(2), col(2))[way]
        if way < 2:
            ref = kv.at[r, c]
        else:
            ref = kv.at[r, c, pl.ds((way - 2) * (rows // 2), rows // 2)]
        return remote(ref, ref, xf_send.at[r, way], xf_recv.at[r, way], (east, west)[way % 2])

    grads.start()

    acc = [jnp.zeros((2 * HALF, rows), F32)]

    def source(r, j):
        c = col(j)
        if r < REACH or j == 0:
            return r, c
        return jnp.where(c < x, 0, REACH), c

    def tile(r, j):
        return 0 if r == 0 else (r - 1) * COLS + j + 1

    def forward(r, j):
        rr, c = source(r, j)
        t = tile(r, j)
        block = kv[rr, c]
        h = jnp.dot(block, qz, preferred_element_type=F32)
        th = jnp.tanh(h)
        u = h * th
        base = ((y - rr) * COLS + c) * rows
        live = key_row >= start - base
        if r == 0:
            live = live & (key_row <= position - base)
        weights = jnp.where(live, h + u, 0.0).astype(BF16)
        pt[t] = weights
        gf[t] = jnp.where(live, (1.0 + th) * (1.0 + (h - u)), 0.0)
        block_t = block.T
        kvt[t] = block_t
        acc[0] = acc[0] + jnp.dot(block_t, weights, preferred_element_type=F32)

    def spread(r):
        if r > 0:
            y_fwd(r - 1).wait_recv()
        if r < REACH:
            y_fwd(r).start()
        x_fwd(r, 0).start()
        x_fwd(r, 1).start()

    def pass_on(r):
        x_fwd_here(r, 0).wait_recv()
        x_fwd(r, 2).start()
        x_fwd_here(r, 1).wait_recv()
        x_fwd(r, 3).start()

    def landed(r):
        x_fwd_here(r, 2).wait_recv()
        x_fwd_here(r, 3).wait_recv()

    spread(0)
    forward(0, 0)
    for r in range(1, REACH + 1):
        spread(r)
        forward(r, 0)
        pass_on(r - 1)
        if r >= 2:
            forward(r - 1, 1)
            forward(r - 1, 3)
            landed(r - 2)
        if r >= 3:
            forward(r - 2, 2)
    pass_on(REACH)
    landed(REACH - 1)
    forward(REACH - 1, 2)
    forward(REACH, 1)
    forward(REACH, 3)
    landed(REACH)
    forward(REACH, 2)

    grads.wait()
    grad_f = grx[...].astype(F32)
    gain = gain_ref[...]
    scaled = grad_f * gain
    both = jnp.concatenate([scaled, scaled * vu[:, HALF:].astype(F32)], axis=1).T
    scaled_t, grad_norm = both[:HALF], both[HALF:]
    attended = acc[0][HALF:] * (1.0 / 256.0)
    sums = jnp.concatenate(
        [
            jnp.sum(value, axis=0, keepdims=True)
            for value in (attended, attended * attended, grad_norm, grad_norm * attended)
        ],
        axis=0,
    )
    stat[z] = jnp.concatenate([sums[:, : rows // 2], sums[:, rows // 2 :]], axis=0)

    def z_copy(k):
        return remote(
            stat.at[z], stat.at[z], z_send.at[k], z_recv.at[k], {"head": (z + k) % heads}
        )

    def z_start(k, carry):
        z_copy(k).start()
        return carry

    def z_wait(k, carry):
        z_copy(k).wait()
        return carry

    lax.fori_loop(1, heads, z_start, 0)
    lax.fori_loop(1, heads, z_wait, 0)
    total = stat[0]
    for k in range(1, heads):
        total = total + stat[k]
    total = jnp.concatenate([total[:4], total[4:]], axis=1) * (1.0 / (HALF * heads))
    mean = total[0:1]
    rsigma = 1.0 / jnp.sqrt(jnp.maximum(total[1:2] - mean * mean, 0.0) + 1e-05)
    one = total[2:3]
    two = (total[3:4] - mean * one) * rsigma
    normed = (attended - mean) * rsigma
    gate_t = scaled_t * normed
    grad_attn = (grad_norm - one - normed * two) * rsigma
    ga_wide = jnp.concatenate([jnp.zeros((HALF, rows), F32), grad_attn], axis=0)
    gaz = ga_wide.astype(BF16)
    ga_right = (ga_wide.T.astype(BF16).astype(F32) * (1.0 / 256.0)).astype(BF16)
    q_left = jnp.where(lane < HALF, qk.astype(F32) * (1.0 / 4096.0), 0.0).astype(BF16)

    dq = [jnp.zeros((2 * HALF, rows), F32)]

    def backward(r, j):
        rr, c = source(r, j)
        t = tile(r, j)
        d_weights = jnp.dot(kv[rr, c], gaz, preferred_element_type=F32)
        ds = (d_weights * gf[t]).astype(BF16)
        dq[0] = dq[0] + jnp.dot(kvt[t], ds, preferred_element_type=F32)
        part = jnp.dot(ds, q_left, preferred_element_type=F32) + jnp.dot(
            pt[t], ga_right, preferred_element_type=F32
        )
        if j == 0:
            own[r] = part
        else:
            psend[r - 1, j - 1] = part.astype(BF16)

    def x_bwd(r, way):
        i = r - 1
        low, high = pl.ds(0, rows // 2), pl.ds(rows // 2, rows // 2)
        src, dst, to = (
            (psend.at[i, 0], precv.at[i, 0], east),
            (psend.at[i, 2], precv.at[i, 2], west),
            (psend.at[i, 1, low], relay.at[i, 0], east),
            (psend.at[i, 1, high], relay.at[i, 1], west),
            (relay.at[i, 0], precv.at[i, 1, low], east),
            (relay.at[i, 1], precv.at[i, 1, high], west),
        )[way]
        return remote(src, dst, xb_send.at[i, way], xb_recv.at[i, way], to)

    def y_bwd(r):
        return remote(ysend.at[r - 1], ych.at[r - 1], yb_send.at[r - 1], yb_recv.at[r - 1], south)

    def tiles(r):
        backward(r, 2)
        x_bwd(r, 2).start()
        x_bwd(r, 3).start()
        backward(r, 1)
        x_bwd(r, 0).start()
        backward(r, 3)
        x_bwd(r, 1).start()
        backward(r, 0)

    def hand_on(r):
        for way in (2, 3):
            x_bwd(r, way).wait_recv()
            x_bwd(r, way + 2).start()

    def collect(r):
        for way in (0, 1, 4, 5):
            x_bwd(r, way).wait_recv()
        found = own[r]
        if r < REACH:
            y_bwd(r + 1).wait_recv()
            found = found + ych[r].astype(F32)
            for j in range(3):
                found = found + precv[r - 1, j].astype(F32)
        else:
            for j in range(3):
                sender = (x + COLS - 1 - j) % COLS
                found = found + jnp.where(sender < x, precv[r - 1, j].astype(F32), 0.0)
        ysend[r - 1] = found.astype(BF16)
        y_bwd(r).start()

    tiles(4)
    tiles(3)
    hand_on(4)
    tiles(2)
    hand_on(3)
    collect(4)
    tiles(1)
    hand_on(2)
    collect(3)
    backward(0, 0)
    hand_on(1)
    collect(2)
    collect(1)
    packed = jnp.concatenate([dq[0][:HALF] * (1.0 / 4096.0), gate_t], axis=0).T
    found = own[0]
    for j in range(3):
        sender = (x + COLS - 1 - j) % COLS
        found = found + jnp.where(sender > x, precv[REACH - 1, j].astype(F32), 0.0)
    y_bwd(1).wait_recv()
    found = found + ych[0].astype(F32)
    found = jnp.concatenate([found[:, HALF:], found[:, :HALF]], axis=1)
    oqk_ref[...] = jnp.where(lane < HALF, packed, found).astype(BF16)
    ovu_ref[...] = jnp.where(lane < HALF, found, packed).astype(BF16)

    for r in range(REACH + 1):
        if r < REACH:
            y_fwd(r).wait_send()
            y_bwd(r + 1).wait_send()
            for way in range(6):
                x_bwd(r + 1, way).wait_send()
        for way in range(4):
            x_fwd(r, way).wait_send()


def body(qk_rows, vu_rows, grad_next, layer_gain, user_lengths):
    rows, wide = qk_rows.shape[1], qk_rows.shape[3]
    heads = lax.axis_size("head")
    tiles = REACH * COLS + 1
    vmem = pl.BlockSpec(memory_space=pltpu.VMEM)
    dma = pltpu.SemaphoreType.DMA
    out = jax.ShapeDtypeStruct((rows, wide), BF16)
    grad_qk, grad_vu = pl.pallas_call(
        kernel,
        out_shape=(out, out),
        in_specs=[vmem, vmem, vmem, vmem, pl.BlockSpec(memory_space=pltpu.SMEM)],
        out_specs=(vmem, vmem),
        scratch_shapes=[
            pltpu.VMEM((REACH + 1, COLS, rows, wide), BF16),
            pltpu.VMEM((tiles, wide, rows), BF16),
            pltpu.VMEM((tiles, rows, rows), BF16),
            pltpu.VMEM((tiles, rows, rows), F32),
            pltpu.VMEM((heads, 8, rows // 2), F32),
            pltpu.VMEM((rows, wide // 2), BF16),
            pltpu.VMEM((REACH, 3, rows, wide), BF16),
            pltpu.VMEM((REACH, 3, rows, wide), BF16),
            pltpu.VMEM((REACH, 2, rows // 2, wide), BF16),
            pltpu.VMEM((REACH, rows, wide), BF16),
            pltpu.VMEM((REACH, rows, wide), BF16),
            pltpu.VMEM((REACH + 1, rows, wide), F32),
            dma((2,)),
            dma((REACH,)),
            dma((REACH,)),
            dma((REACH + 1, 4)),
            dma((REACH + 1, 4)),
            dma((heads,)),
            dma((heads,)),
            dma((REACH, 6)),
            dma((REACH, 6)),
            dma((REACH,)),
            dma((REACH,)),
        ],
        compiler_params=pltpu.CompilerParams(
            collective_id=0, has_side_effects=True, vmem_limit_bytes=50 * 1024 * 1024
        ),
        name="attention_backward",
    )(
        qk_rows.reshape(rows, wide),
        vu_rows.reshape(rows, wide),
        grad_next.reshape(rows, wide // 2),
        layer_gain,
        user_lengths,
    )
    return grad_qk.reshape(1, rows, 1, wide), grad_vu.reshape(1, rows, 1, wide)


def solution(mesh):
    split = P("pipe", "seq", "head", None)
    return jax.shard_map(
        body,
        mesh=mesh,
        in_specs=(split, split, split, P("head", None), P("pipe", None)),
        out_specs=(split, split),
        check_vma=False,
    )
```

```python
import jax
import jax.numpy as jnp
from jax import lax
from jax.experimental import pallas as pl
from jax.experimental.pallas import tpu as pltpu
from jax.sharding import PartitionSpec as P

MESH = pl.DeviceIdType.MESH
F32 = jnp.float32
BF16 = jnp.bfloat16
COLS = 4
REACH = 4
HALF = 64
CHUNKS = 4


def kernel(
    qk_ref, vu_ref, gr_ref, gain_ref, len_ref,
    oqk_ref, ovu_ref,
    kv, kvt, pt, gf, pk, gk, qt, gat, stat, grx,
    g_sem, kvy_send, kvy_recv, kvx_send, kvx_recv, qy_send, qy_recv, qx_send, qx_recv,
    gy_send, gy_recv, gx_send, gx_recv, z_send, z_recv,
):
    rows = qk_ref.shape[0]
    seqs = lax.axis_size("seq")
    heads = lax.axis_size("head")
    s, z, core = lax.axis_index("seq"), lax.axis_index("head"), lax.axis_index("pipe")
    x, y = s % COLS, s // COLS
    tall = seqs // COLS

    def col(j):
        return (x + j) % COLS

    def up(by):
        return {"seq": ((y + tall + by) % tall) * COLS + x}

    east = {"seq": y * COLS + col(1)}
    west = {"seq": y * COLS + col(COLS - 1)}
    partner = {"pipe": 1 - core}

    def remote(src, dst, send, recv, to):
        return pltpu.make_async_remote_copy(
            src_ref=src, dst_ref=dst, send_sem=send, recv_sem=recv, device_id=to, device_id_type=MESH
        )

    barrier = pltpu.get_barrier_semaphore()
    near = (east, west, up(1), up(-1), up(2), up(-2), partner)
    for to in near:
        pl.semaphore_signal(barrier, inc=1, device_id=to, device_id_type=MESH)

    def greet(k, carry):
        pl.semaphore_signal(barrier, inc=1, device_id={"head": (z + k) % heads}, device_id_type=MESH)
        return carry

    lax.fori_loop(1, heads, greet, 0)

    qk = qk_ref[...]
    vu = vu_ref[...]
    keys = qk[:, HALF:]
    values = vu[:, :HALF]
    kv[0, x] = jnp.concatenate([keys, values], axis=1)
    sub = lax.broadcasted_iota(jnp.int32, (2 * HALF, rows), 0)
    qk_t = qk.astype(F32).T
    qz = jnp.where(sub < HALF, qk_t * (0.5 * HALF ** -0.5), 0.0).astype(BF16)
    qt[0, x] = qk_t[:HALF].astype(BF16)
    keys_small = (keys.astype(F32) * (0.5 * HALF ** -0.5)).astype(BF16)
    gate_in = vu.astype(F32).T[HALF:]
    gain = jnp.broadcast_to(gain_ref[...], (2 * HALF, HALF)).T[:, :1]
    ends = [len_ref[0, 0]]
    for user in range(1, len_ref.shape[1]):
        ends.append(ends[-1] + len_ref[0, user])
    offset = lax.broadcasted_iota(jnp.int32, (1, rows), 1)

    def first_of(position):
        start = jnp.zeros((1, rows), jnp.int32)
        for end in ends:
            start = jnp.where(position >= end, end, start)
        return start

    start = first_of(s * rows + offset)
    key_row = lax.broadcasted_iota(jnp.int32, (rows, rows), 0)

    pl.semaphore_wait(barrier, heads - 1 + len(near))

    def ring(buf, send, recv):
        half = buf.shape[2] // 2
        low, high = pl.ds(0, half), pl.ds(half, half)
        parts = (low, low, high, high, low, high)

        def sent(r, way):
            c = (x, x, x, x, col(COLS - 1), col(1))[way]
            ref = buf.at[r, c, parts[way]]
            return remote(ref, ref, send.at[r, way], recv.at[r, way], (east, west)[way % 2])

        def got(r, way):
            c = (col(COLS - 1), col(1), col(COLS - 1), col(1), col(2), col(2))[way]
            ref = buf.at[r, c, parts[way]]
            return remote(ref, ref, send.at[r, way], recv.at[r, way], (east, west)[way % 2])

        return sent, got

    kv_sent, kv_got = ring(kv, kvx_send, kvx_recv)
    q_sent, q_got = ring(qt, qx_send, qx_recv)
    g_sent, g_got = ring(gat, gx_send, gx_recv)

    def pass_on(ring_sent, ring_got, r):
        ring_got(r, 0).wait_recv()
        ring_sent(r, 4).start()
        ring_got(r, 1).wait_recv()
        ring_got(r, 3).wait_recv()
        ring_sent(r, 5).start()
        ring_got(r, 2).wait_recv()

    def landed(ring_got, r):
        ring_got(r, 4).wait_recv()
        ring_got(r, 5).wait_recv()

    chunk = rows // CHUNKS

    def kv_north(r, part):
        piece = pl.ds(part * chunk, chunk)
        return remote(
            kv.at[r, x, piece], kv.at[r + 1, x, piece], kvy_send.at[r, part], kvy_recv.at[r, part], up(1)
        )

    def q_south(r):
        return remote(qt.at[r, x], qt.at[r + 1, x], qy_send.at[r], qy_recv.at[r], up(-1))

    def g_south(r):
        return remote(
            gat.at[(r - 1) // 2 * 2, x], gat.at[r, x], gy_send.at[r - 1], gy_recv.at[r - 1], up(-2 + r % 2)
        )

    grads = remote(gr_ref, grx, g_sem.at[0], g_sem.at[1], partner)

    acc = [jnp.zeros((2 * HALF, rows), F32)]
    dq = [jnp.zeros((2 * HALF, rows), F32)]
    dk = [jnp.zeros((rows, HALF), F32)]
    dv = [jnp.zeros((rows, HALF), F32)]

    def tile(r, j):
        return 0 if r == 0 else (r - 1) * COLS + j + 1

    def behind(r, j):
        c = col(j)
        return (r, c) if r < REACH or j == 0 else (jnp.where(c < x, 0, REACH), c)

    def ahead(r, j):
        c = col(j)
        return (r, c) if r < REACH or j == 0 else (jnp.where(c > x, 0, REACH), c)

    def gated(h, live):
        th = jnp.tanh(h)
        u = h * th
        weights = jnp.where(live, h + u, 0.0).astype(BF16)
        return weights, jnp.where(live, (1.0 + th) * (1.0 + (h - u)), 0.0)

    def forward(r, j):
        rr, c = behind(r, j)
        t = tile(r, j)
        block = kv[rr, c]
        h = jnp.dot(block, qz, preferred_element_type=F32)
        base = ((y - rr) * COLS + c) * rows
        live = key_row >= start - base
        if r == 0:
            live = live & (key_row <= offset)
        weights, factor = gated(h, live)
        pt[t] = weights
        gf[t] = factor
        block_t = block.T
        kvt[t] = block_t
        acc[0] = acc[0] + jnp.dot(block_t, weights, preferred_element_type=F32)

    def key_side(r, j):
        rr, c = ahead(r, j)
        t = tile(r, j) - 1
        h = jnp.dot(keys_small, qt[rr, c], preferred_element_type=F32)
        live = key_row >= first_of(((y + rr) * COLS + c) * rows + offset) - s * rows
        pk[t], gk[t] = gated(h, live)

    def into_keys(ds, weights, queries, grad):
        nt = (((1,), (1,)), ((), ()))
        dk[0] = dk[0] + lax.dot_general(ds, queries, nt, preferred_element_type=F32)
        dv[0] = dv[0] + lax.dot_general(weights, grad, nt, preferred_element_type=F32)

    def spread(r):
        for half in range(2):
            for part in range(half * CHUNKS // 2, (half + 1) * CHUNKS // 2):
                if r > 0:
                    kv_north(r - 1, part).wait_recv()
                if r < REACH:
                    kv_north(r, part).start()
            kv_sent(r, 2 * half).start()
            kv_sent(r, 2 * half + 1).start()

    spread(0)
    q_south(0).start()
    grads.start()
    forward(0, 0)
    for r in range(1, REACH + 1):
        spread(r)
        forward(r, 0)
        pass_on(kv_sent, kv_got, r - 1)
        if r >= 2:
            forward(r - 1, 1)
            forward(r - 1, 3)
            landed(kv_got, r - 2)
        if r >= 3:
            forward(r - 2, 2)
        q_south(r - 1).wait_recv()
        if r < REACH:
            q_south(r).start()
    pass_on(kv_sent, kv_got, REACH)
    for r in range(REACH + 1):
        for way in range(4):
            q_sent(r, way).start()
    landed(kv_got, REACH - 1)
    forward(REACH - 1, 2)
    forward(REACH, 1)
    forward(REACH, 3)
    grads.wait()
    scaled = grx[...].astype(F32) * gain
    grad_norm = scaled * gate_in
    landed(kv_got, REACH)
    forward(REACH, 2)

    attended = acc[0][HALF:] * (1.0 / 256.0)
    sums = jnp.concatenate(
        [
            jnp.sum(value, axis=0, keepdims=True)
            for value in (attended, attended * attended, grad_norm, grad_norm * attended)
        ],
        axis=0,
    )
    stat[z] = jnp.concatenate([sums[:, : rows // 2], sums[:, rows // 2 :]], axis=0)

    def z_copy(k):
        return remote(
            stat.at[z], stat.at[z], z_send.at[k], z_recv.at[k], {"head": (z + k) % heads}
        )

    def z_start(k, carry):
        z_copy(k).start()
        return carry

    def z_wait(k, carry):
        z_copy(k).wait()
        return carry

    lax.fori_loop(1, heads, z_start, 0)
    for r in range(REACH + 1):
        pass_on(q_sent, q_got, r)
    lax.fori_loop(1, heads, z_wait, 0)
    total = stat[0]
    for k in range(1, heads):
        total = total + stat[k]
    total = jnp.concatenate([total[:4], total[4:]], axis=1) * (1.0 / (HALF * heads))
    mean = total[0:1]
    rsigma = 1.0 / jnp.sqrt(jnp.maximum(total[1:2] - mean * mean, 0.0) + 1e-05)
    one = total[2:3]
    two = (total[3:4] - mean * one) * rsigma
    normed = (attended - mean) * rsigma
    grad_attn = ((grad_norm - one - normed * two) * rsigma).astype(BF16)
    gat[0, x] = grad_attn

    g_south(2).start()
    g_south(1).start()
    for way in range(4):
        g_sent(0, way).start()
    gate = scaled * normed
    gaz = jnp.concatenate([jnp.zeros((HALF, rows), BF16), grad_attn], axis=0)

    def query_side(r, j):
        rr, c = behind(r, j)
        t = tile(r, j)
        d_weights = jnp.dot(kv[rr, c], gaz, preferred_element_type=F32)
        ds = (d_weights * gf[t]).astype(BF16)
        dq[0] = dq[0] + jnp.dot(kvt[t], ds, preferred_element_type=F32)
        if r == 0:
            into_keys(ds, pt[0], qt[0, x], grad_attn)

    def key_grads(r, j):
        rr, c = ahead(r, j)
        t = tile(r, j) - 1
        grad = gat[rr, c]
        ds = (jnp.dot(values, grad, preferred_element_type=F32) * gk[t]).astype(BF16)
        into_keys(ds, pk[t], qt[rr, c], grad)

    def g_spread(r):
        g_south(r).wait_recv()
        if r == 2:
            g_south(4).start()
            g_south(3).start()
        for way in range(4):
            g_sent(r, way).start()

    for r in range(REACH + 1):
        landed(q_got, r)
    query_side(0, 0)
    for r in (1, 2):
        for j in range(COLS):
            query_side(r, j)
    g_spread(2)
    g_spread(1)
    pass_on(g_sent, g_got, 0)
    for r in (3, 4):
        for j in range(COLS):
            query_side(r, j)
    for r in (1, 2):
        for j in range(COLS):
            key_side(r, j)
    pass_on(g_sent, g_got, 2)
    pass_on(g_sent, g_got, 1)
    for r in (3, 4):
        for j in range(COLS):
            key_side(r, j)
    g_spread(3)
    g_spread(4)
    for r in (1, 2):
        for j in (0, 1, 3):
            key_grads(r, j)
    for r in (0, 2, 1):
        landed(g_got, r)
    key_grads(2, 2)
    key_grads(1, 2)
    pass_on(g_sent, g_got, 3)
    pass_on(g_sent, g_got, 4)
    for r in (3, 4):
        for j in (0, 1, 3):
            key_grads(r, j)
    packed = jnp.concatenate([dq[0][:HALF] * (1.0 / 4096.0), gate], axis=0).T
    landed(g_got, 3)
    key_grads(3, 2)
    landed(g_got, 4)
    key_grads(4, 2)
    oqk_ref[...] = jnp.concatenate([packed[:, :HALF], dk[0] * (1.0 / 4096.0)], axis=1).astype(BF16)
    ovu_ref[...] = jnp.concatenate([dv[0] * (1.0 / 256.0), packed[:, HALF:]], axis=1).astype(BF16)

    for r in range(REACH):
        for part in range(CHUNKS):
            kv_north(r, part).wait_send()
        q_south(r).wait_send()
        g_south(r + 1).wait_send()
    for r in range(REACH + 1):
        for way in range(6):
            kv_sent(r, way).wait_send()
            q_sent(r, way).wait_send()
            g_sent(r, way).wait_send()


def body(qk_rows, vu_rows, grad_next, layer_gain, user_lengths):
    rows, wide = qk_rows.shape[1], qk_rows.shape[3]
    heads = lax.axis_size("head")
    tiles = REACH * COLS + 1
    vmem = pl.BlockSpec(memory_space=pltpu.VMEM)
    dma = pltpu.SemaphoreType.DMA
    out = jax.ShapeDtypeStruct((rows, wide), BF16)
    grad_qk, grad_vu = pl.pallas_call(
        kernel,
        out_shape=(out, out),
        in_specs=[vmem, vmem, vmem, vmem, pl.BlockSpec(memory_space=pltpu.SMEM)],
        out_specs=(vmem, vmem),
        scratch_shapes=[
            pltpu.VMEM((REACH + 1, COLS, rows, wide), BF16),
            pltpu.VMEM((tiles, wide, rows), BF16),
            pltpu.VMEM((tiles, rows, rows), BF16),
            pltpu.VMEM((tiles, rows, rows), F32),
            pltpu.VMEM((tiles - 1, rows, rows), BF16),
            pltpu.VMEM((tiles - 1, rows, rows), F32),
            pltpu.VMEM((REACH + 1, COLS, wide // 2, rows), BF16),
            pltpu.VMEM((REACH + 1, COLS, wide // 2, rows), BF16),
            pltpu.VMEM((heads, 8, rows // 2), F32),
            pltpu.VMEM((wide // 2, rows), BF16),
            dma((2,)),
            dma((REACH, CHUNKS)),
            dma((REACH, CHUNKS)),
            dma((REACH + 1, 6)),
            dma((REACH + 1, 6)),
            dma((REACH,)),
            dma((REACH,)),
            dma((REACH + 1, 6)),
            dma((REACH + 1, 6)),
            dma((REACH,)),
            dma((REACH,)),
            dma((REACH + 1, 6)),
            dma((REACH + 1, 6)),
            dma((heads,)),
            dma((heads,)),
        ],
        compiler_params=pltpu.CompilerParams(
            collective_id=0, has_side_effects=True, vmem_limit_bytes=50 * 1024 * 1024
        ),
        name="attention_backward",
    )(
        qk_rows.reshape(rows, wide),
        vu_rows.reshape(rows, wide),
        grad_next.reshape(rows, wide // 2).T,
        layer_gain,
        user_lengths,
    )
    return grad_qk.reshape(1, rows, 1, wide), grad_vu.reshape(1, rows, 1, wide)


def solution(mesh):
    split = P("pipe", "seq", "head", None)
    return jax.shard_map(
        body,
        mesh=mesh,
        in_specs=(split, split, split, P("head", None), P("pipe", None)),
        out_specs=(split, split),
        check_vma=False,
    )
```

```python
import jax
import jax.numpy as jnp
from jax import lax
from jax.experimental import pallas as pl
from jax.experimental.pallas import tpu as pltpu
from jax.sharding import PartitionSpec as P

MESH = pl.DeviceIdType.MESH
F32 = jnp.float32
BF16 = jnp.bfloat16
COLS = 4
REACH = 4
HALF = 64
CHUNKS = 4
VMEM_BYTES = 67043328


def kernel(
    qk_ref, vu_ref, gr_ref, gain_ref, len_ref,
    oqk_ref, ovu_ref,
    kv, kvt, pt, gf, pk, gk, qt, gat, stat, grx,
    qk_in, vu_in, gr_in, in_sem, word, g_sem, kvy_send, kvy_recv, kvx_send, kvx_recv, qy_send, qy_recv, qx_send, qx_recv,
    gy_send, gy_recv, gx_send, gx_recv, z_send, z_recv,
):
    rows = qk_ref.shape[0]
    seqs = lax.axis_size("seq")
    heads = lax.axis_size("head")
    s, z, core = lax.axis_index("seq"), lax.axis_index("head"), lax.axis_index("pipe")
    x, y = s % COLS, s // COLS
    tall = seqs // COLS

    def col(j):
        return (x + j) % COLS

    def up(by):
        return {"seq": ((y + tall + by) % tall) * COLS + x}

    east = {"seq": y * COLS + col(1)}
    west = {"seq": y * COLS + col(COLS - 1)}
    partner = {"pipe": 1 - core}

    def remote(src, dst, send, recv, to):
        return pltpu.make_async_remote_copy(
            src_ref=src, dst_ref=dst, send_sem=send, recv_sem=recv, device_id=to, device_id_type=MESH
        )

    barrier = pltpu.get_barrier_semaphore()
    above, below = {"head": (z + 1) % heads}, {"head": (z + heads - 1) % heads}
    near = (east, west, up(1), up(-1), up(2), up(-2), partner, above, below)
    for to in near:
        pl.semaphore_signal(barrier, inc=1, device_id=to, device_id_type=MESH)

    loads = [
        pltpu.make_async_copy(src, dst, in_sem.at[i])
        for i, (src, dst) in enumerate(((qk_ref, qk_in), (vu_ref, vu_in), (gr_ref, gr_in)))
    ]
    for load in loads:
        load.start()
    loads[0].wait()
    loads[1].wait()
    qk = qk_in[...]
    vu = vu_in[...]
    lane = lax.broadcasted_iota(jnp.int32, (rows, 2 * HALF), 1)
    kv[0, x] = jnp.where(lane < HALF, vu, qk)
    pl.semaphore_wait(barrier, len(near))

    def say(i):
        pl.semaphore_signal(word.at[0, i], inc=1, device_id=above, device_id_type=MESH)
        pl.semaphore_signal(word.at[1, i], inc=1, device_id=below, device_id_type=MESH)

    def hear(i):
        pl.semaphore_wait(word.at[0, i], 1)
        pl.semaphore_wait(word.at[1, i], 1)

    words = heads // 2 - 1
    say(0)

    def ring(buf, send, recv):
        half = buf.shape[2] // 2
        low, high = pl.ds(0, half), pl.ds(half, half)
        parts = (low, low, high, high, low, high)

        def sent(r, way):
            c = (x, x, x, x, col(COLS - 1), col(1))[way]
            ref = buf.at[r, c, parts[way]]
            return remote(ref, ref, send.at[r, way], recv.at[r, way], (east, west)[way % 2])

        def got(r, way):
            c = (col(COLS - 1), col(1), col(COLS - 1), col(1), col(2), col(2))[way]
            ref = buf.at[r, c, parts[way]]
            return remote(ref, ref, send.at[r, way], recv.at[r, way], (east, west)[way % 2])

        return sent, got

    kv_sent, kv_got = ring(kv, kvx_send, kvx_recv)
    q_sent, q_got = ring(qt, qx_send, qx_recv)
    g_sent, g_got = ring(gat, gx_send, gx_recv)

    def pass_on(ring_sent, ring_got, r):
        ring_got(r, 0).wait_recv()
        ring_sent(r, 4).start()
        ring_got(r, 1).wait_recv()
        ring_got(r, 3).wait_recv()
        ring_sent(r, 5).start()
        ring_got(r, 2).wait_recv()

    def landed(ring_got, r):
        ring_got(r, 4).wait_recv()
        ring_got(r, 5).wait_recv()

    chunk = rows // CHUNKS

    def kv_north(r, part):
        piece = pl.ds(part * chunk, chunk)
        return remote(
            kv.at[r, x, piece], kv.at[r + 1, x, piece], kvy_send.at[r, part], kvy_recv.at[r, part], up(1)
        )

    def q_south(r):
        return remote(qt.at[r, x], qt.at[r + 1, x], qy_send.at[r], qy_recv.at[r], up(-1))

    def g_south(r):
        return remote(
            gat.at[(r - 1) // 2 * 2, x], gat.at[r, x], gy_send.at[r - 1], gy_recv.at[r - 1], up(-2 + r % 2)
        )

    grads = remote(gr_in, grx, g_sem.at[0], g_sem.at[1], partner)

    acc = [jnp.zeros((2 * HALF, rows), F32)]
    dq = [jnp.zeros((2 * HALF, rows), F32)]
    dk = [jnp.zeros((rows, HALF), F32)]
    dv = [jnp.zeros((rows, HALF), F32)]

    def tile(r, j):
        return 0 if r == 0 else (r - 1) * COLS + j + 1

    def behind(r, j):
        c = col(j)
        return (r, c) if r < REACH or j == 0 else (jnp.where(c < x, 0, REACH), c)

    def ahead(r, j):
        c = col(j)
        return (r, c) if r < REACH or j == 0 else (jnp.where(c > x, 0, REACH), c)

    def gated(h, live):
        th = jnp.tanh(h)
        u = h * th
        weights = jnp.where(live, h + u, 0.0).astype(BF16)
        return weights, jnp.where(live, (1.0 + th) * (1.0 + (h - u)), 0.0)

    def forward(r, j):
        rr, c = behind(r, j)
        t = tile(r, j)
        block = kv[rr, c]
        h = jnp.dot(block, qz, preferred_element_type=F32)
        base = ((y - rr) * COLS + c) * rows
        live = key_row >= start - base
        if r == 0:
            live = live & (key_row <= offset)
        weights, factor = gated(h, live)
        pt[t] = weights
        gf[t] = factor
        block_t = block.T
        kvt[t] = block_t
        acc[0] = acc[0] + jnp.dot(block_t, weights, preferred_element_type=F32)

    def key_side(r, j):
        rr, c = ahead(r, j)
        t = tile(r, j) - 1
        h = jnp.dot(keys_small, qt[rr, c], preferred_element_type=F32)
        live = key_row >= first_of(((y + rr) * COLS + c) * rows + offset) - s * rows
        pk[t], gk[t] = gated(h, live)

    def into_keys(ds, weights, queries, grad):
        nt = (((1,), (1,)), ((), ()))
        dk[0] = dk[0] + lax.dot_general(ds, queries, nt, preferred_element_type=F32)
        dv[0] = dv[0] + lax.dot_general(weights, grad, nt, preferred_element_type=F32)

    def spread(r):
        for half in range(2):
            for part in range(half * CHUNKS // 2, (half + 1) * CHUNKS // 2):
                if r > 0:
                    kv_north(r - 1, part).wait_recv()
                if r < REACH:
                    kv_north(r, part).start()
            kv_sent(r, 2 * half).start()
            kv_sent(r, 2 * half + 1).start()

    spread(0)
    loads[2].wait()
    grads.start()
    keys = qk[:, HALF:]
    values = vu[:, :HALF]
    qk_t = qk.astype(F32).T
    no_rows = jnp.zeros((HALF, rows), BF16)
    qz = jnp.concatenate([no_rows, (qk_t[:HALF] * (0.5 * HALF ** -0.5)).astype(BF16)], axis=0)
    qt[0, x] = qk_t[:HALF].astype(BF16)
    keys_small = (keys.astype(F32) * (0.5 * HALF ** -0.5)).astype(BF16)
    gate_in = vu.astype(F32).T[HALF:]
    gain = jnp.broadcast_to(gain_ref[...], (2 * HALF, HALF)).T[:, :1]
    ends = [len_ref[0, 0]]
    for user in range(1, len_ref.shape[1]):
        ends.append(ends[-1] + len_ref[0, user])
    offset = lax.broadcasted_iota(jnp.int32, (1, rows), 1)

    def first_of(position):
        start = jnp.zeros((1, rows), jnp.int32)
        for end in ends:
            start = jnp.where(position >= end, end, start)
        return start

    start = first_of(s * rows + offset)
    key_row = lax.broadcasted_iota(jnp.int32, (rows, rows), 0)

    q_south(0).start()
    forward(0, 0)
    for r in range(1, REACH + 1):
        spread(r)
        forward(r, 0)
        pass_on(kv_sent, kv_got, r - 1)
        if r >= 2:
            forward(r - 1, 1)
            forward(r - 1, 3)
            landed(kv_got, r - 2)
        if r >= 3:
            forward(r - 2, 2)
        q_south(r - 1).wait_recv()
        if r < REACH:
            q_south(r).start()
        if r < words:
            hear(r - 1)
            say(r)
    pass_on(kv_sent, kv_got, REACH)
    for r in range(REACH + 1):
        for way in range(4):
            q_sent(r, way).start()
    landed(kv_got, REACH - 1)
    forward(REACH - 1, 2)
    forward(REACH, 1)
    forward(REACH, 3)
    grads.wait()
    scaled = grx[...].astype(F32) * gain
    grad_norm = scaled * gate_in
    landed(kv_got, REACH)
    forward(REACH, 2)

    attended = acc[0][:HALF] * (1.0 / 256.0)
    sums = jnp.concatenate(
        [
            jnp.sum(value, axis=0, keepdims=True)
            for value in (attended, attended * attended, grad_norm, grad_norm * attended)
        ],
        axis=0,
    )
    stat[z] = jnp.concatenate([sums[:, : rows // 2], sums[:, rows // 2 :]], axis=0)

    def z_copy(k):
        return remote(
            stat.at[z], stat.at[z], z_send.at[k], z_recv.at[k], {"head": (z + k) % heads}
        )

    def z_start(k, carry):
        z_copy(k).start()
        return carry

    def z_wait(k, carry):
        z_copy(k).wait()
        return carry

    for i in range(min(words, REACH + 1) - 1, words):
        hear(i)
        if i + 1 < words:
            say(i + 1)
    lax.fori_loop(1, heads, z_start, 0)
    for r in range(REACH + 1):
        pass_on(q_sent, q_got, r)
    lax.fori_loop(1, heads, z_wait, 0)
    total = stat[0]
    for k in range(1, heads):
        total = total + stat[k]
    total = jnp.concatenate([total[:4], total[4:]], axis=1) * (1.0 / (HALF * heads))
    mean = total[0:1]
    rsigma = 1.0 / jnp.sqrt(jnp.maximum(total[1:2] - mean * mean, 0.0) + 1e-05)
    one = total[2:3]
    two = (total[3:4] - mean * one) * rsigma
    normed = (attended - mean) * rsigma
    grad_attn = ((grad_norm - one - normed * two) * rsigma).astype(BF16)
    gat[0, x] = grad_attn

    g_south(2).start()
    g_south(1).start()
    for way in range(4):
        g_sent(0, way).start()
    gate = scaled * normed
    gaz = jnp.concatenate([grad_attn, no_rows], axis=0)

    def query_side(r, j):
        rr, c = behind(r, j)
        t = tile(r, j)
        d_weights = jnp.dot(kv[rr, c], gaz, preferred_element_type=F32)
        ds = (d_weights * gf[t]).astype(BF16)
        dq[0] = dq[0] + jnp.dot(kvt[t], ds, preferred_element_type=F32)
        if r == 0:
            into_keys(ds, pt[0], qt[0, x], grad_attn)

    def key_grads(r, j):
        rr, c = ahead(r, j)
        t = tile(r, j) - 1
        grad = gat[rr, c]
        ds = (jnp.dot(values, grad, preferred_element_type=F32) * gk[t]).astype(BF16)
        into_keys(ds, pk[t], qt[rr, c], grad)

    def g_spread(r):
        g_south(r).wait_recv()
        if r == 2:
            g_south(4).start()
            g_south(3).start()
        for way in range(4):
            g_sent(r, way).start()

    for r in range(REACH + 1):
        landed(q_got, r)
    query_side(0, 0)
    for r in (1, 2):
        for j in range(COLS):
            query_side(r, j)
    g_spread(2)
    g_spread(1)
    pass_on(g_sent, g_got, 0)
    for r in (3, 4):
        for j in range(COLS):
            query_side(r, j)
    for r in (1, 2):
        for j in range(COLS):
            key_side(r, j)
    pass_on(g_sent, g_got, 2)
    pass_on(g_sent, g_got, 1)
    for r in (3, 4):
        for j in range(COLS):
            key_side(r, j)
    g_spread(3)
    g_spread(4)
    for r in (1, 2):
        for j in (0, 1, 3):
            key_grads(r, j)
    for r in (0, 2, 1):
        landed(g_got, r)
    key_grads(2, 2)
    key_grads(1, 2)
    pass_on(g_sent, g_got, 3)
    pass_on(g_sent, g_got, 4)
    for r in (3, 4):
        for j in (0, 1, 3):
            key_grads(r, j)
    packed = jnp.concatenate([dq[0][HALF:] * (1.0 / 4096.0), gate], axis=0).T
    landed(g_got, 3)
    key_grads(3, 2)
    landed(g_got, 4)
    key_grads(4, 2)
    oqk_ref[...] = jnp.concatenate([packed[:, :HALF], dk[0] * (1.0 / 4096.0)], axis=1).astype(BF16)
    ovu_ref[...] = jnp.concatenate([dv[0] * (1.0 / 256.0), packed[:, HALF:]], axis=1).astype(BF16)

    for r in range(REACH):
        for part in range(CHUNKS):
            kv_north(r, part).wait_send()
        q_south(r).wait_send()
        g_south(r + 1).wait_send()
    for r in range(REACH + 1):
        for way in range(6):
            kv_sent(r, way).wait_send()
            q_sent(r, way).wait_send()
            g_sent(r, way).wait_send()


def body(qk_rows, vu_rows, grad_next, layer_gain, user_lengths):
    rows, wide = qk_rows.shape[1], qk_rows.shape[3]
    heads = lax.axis_size("head")
    tiles = REACH * COLS + 1
    vmem = pl.BlockSpec(memory_space=pltpu.VMEM)
    hbm = pl.BlockSpec(memory_space=pltpu.HBM)
    dma = pltpu.SemaphoreType.DMA
    out = jax.ShapeDtypeStruct((rows, wide), BF16)
    grad_qk, grad_vu = pl.pallas_call(
        kernel,
        out_shape=(out, out),
        in_specs=[hbm, hbm, hbm, vmem, pl.BlockSpec(memory_space=pltpu.SMEM)],
        out_specs=(vmem, vmem),
        scratch_shapes=[
            pltpu.VMEM((REACH + 1, COLS, rows, wide), BF16),
            pltpu.VMEM((tiles, wide, rows), BF16),
            pltpu.VMEM((tiles, rows, rows), BF16),
            pltpu.VMEM((tiles, rows, rows), F32),
            pltpu.VMEM((tiles - 1, rows, rows), BF16),
            pltpu.VMEM((tiles - 1, rows, rows), F32),
            pltpu.VMEM((REACH + 1, COLS, wide // 2, rows), BF16),
            pltpu.VMEM((REACH + 1, COLS, wide // 2, rows), BF16),
            pltpu.VMEM((heads, 8, rows // 2), F32),
            pltpu.VMEM((wide // 2, rows), BF16),
            pltpu.VMEM((rows, wide), BF16),
            pltpu.VMEM((rows, wide), BF16),
            pltpu.VMEM((wide // 2, rows), BF16),
            dma((3,)),
            pltpu.SemaphoreType.REGULAR((2, heads // 2 - 1)),
            dma((2,)),
            dma((REACH, CHUNKS)),
            dma((REACH, CHUNKS)),
            dma((REACH + 1, 6)),
            dma((REACH + 1, 6)),
            dma((REACH,)),
            dma((REACH,)),
            dma((REACH + 1, 6)),
            dma((REACH + 1, 6)),
            dma((REACH,)),
            dma((REACH,)),
            dma((REACH + 1, 6)),
            dma((REACH + 1, 6)),
            dma((heads,)),
            dma((heads,)),
        ],
        compiler_params=pltpu.CompilerParams(
            collective_id=0, has_side_effects=True, vmem_limit_bytes=VMEM_BYTES
        ),
        name="attention_backward",
    )(
        qk_rows.reshape(rows, wide),
        vu_rows.reshape(rows, wide),
        grad_next.reshape(rows, wide // 2).T,
        layer_gain,
        user_lengths,
    )
    return grad_qk.reshape(1, rows, 1, wide), grad_vu.reshape(1, rows, 1, wide)


def solution(mesh):
    split = P("pipe", "seq", "head", None)
    return jax.shard_map(
        body,
        mesh=mesh,
        in_specs=(split, split, split, P("head", None), P("pipe", None)),
        out_specs=(split, split),
        check_vma=False,
    )
```

```python
import jax
import jax.numpy as jnp
from jax import lax
from jax.experimental import pallas as pl
from jax.experimental.pallas import tpu as pltpu
from jax.sharding import PartitionSpec as P

MESH = pl.DeviceIdType.MESH
F32 = jnp.float32
BF16 = jnp.bfloat16
COLS = 4
REACH = 4
HALF = 64
CHUNKS = 4
VMEM_BYTES = 67043328


class Guarded:
    def __init__(self, copy, when):
        self.copy, self.when = copy, when

    def start(self):
        pl.when(self.when)(self.copy.start)

    def wait_send(self):
        pl.when(self.when)(self.copy.wait_send)

    def wait_recv(self):
        pl.when(self.when)(self.copy.wait_recv)


def only(copy, r, way, at, early):
    if 0 < r < REACH:
        return copy
    if (r == 0) == early:
        when = (at <= 2, at == 0, at <= 2, at <= 1, (at == 1) | (at == 2), (at == 3) | (at == 0))[way]
    else:
        when = (at >= 2, at >= 1, at == 3, at >= 1, (at == 3) | (at == 0), (at == 1) | (at == 2))[way]
    return Guarded(copy, when)


def kernel(
    qk_ref, vu_ref, gr_ref, gain_ref, len_ref,
    oqk_ref, ovu_ref,
    kv, kvt, pt, gf, pk, gk, qt, gat, stat, grx,
    qk_in, vu_in, gr_in, in_sem, word, g_sem, kvy_send, kvy_recv, kvx_send, kvx_recv, qy_send, qy_recv, qx_send, qx_recv,
    gy_send, gy_recv, gx_send, gx_recv, z_send, z_recv,
):
    rows = qk_ref.shape[0]
    seqs = lax.axis_size("seq")
    heads = lax.axis_size("head")
    s, z, core = lax.axis_index("seq"), lax.axis_index("head"), lax.axis_index("pipe")
    x, y = s % COLS, s // COLS
    tall = seqs // COLS

    def col(j):
        return (x + j) % COLS

    def up(by):
        return {"seq": ((y + tall + by) % tall) * COLS + x}

    east = {"seq": y * COLS + col(1)}
    west = {"seq": y * COLS + col(COLS - 1)}
    partner = {"pipe": 1 - core}

    def remote(src, dst, send, recv, to):
        return pltpu.make_async_remote_copy(
            src_ref=src, dst_ref=dst, send_sem=send, recv_sem=recv, device_id=to, device_id_type=MESH
        )

    barrier = pltpu.get_barrier_semaphore()
    above, below = {"head": (z + 1) % heads}, {"head": (z + heads - 1) % heads}
    near = (east, west, up(1), up(-1), up(2), up(-2), partner, above, below)
    for to in near:
        pl.semaphore_signal(barrier, inc=1, device_id=to, device_id_type=MESH)

    loads = [
        pltpu.make_async_copy(src, dst, in_sem.at[i])
        for i, (src, dst) in enumerate(((qk_ref, qk_in), (vu_ref, vu_in), (gr_ref, gr_in)))
    ]
    for load in loads:
        load.start()
    loads[0].wait()
    loads[1].wait()
    qk = qk_in[...]
    vu = vu_in[...]
    lane = lax.broadcasted_iota(jnp.int32, (rows, 2 * HALF), 1)
    kv[0, x] = jnp.where(lane < HALF, vu, qk)
    pl.semaphore_wait(barrier, len(near))

    def say(i):
        pl.semaphore_signal(word.at[0, i], inc=1, device_id=above, device_id_type=MESH)
        pl.semaphore_signal(word.at[1, i], inc=1, device_id=below, device_id_type=MESH)

    def hear(i):
        pl.semaphore_wait(word.at[0, i], 1)
        pl.semaphore_wait(word.at[1, i], 1)

    words = heads // 2 - 1
    say(0)

    def ring(buf, send, recv, early):
        half = buf.shape[2] // 2
        low, high = pl.ds(0, half), pl.ds(half, half)
        parts = (low, low, high, high, low, high)

        def sent(r, way):
            c = (x, x, x, x, col(COLS - 1), col(1))[way]
            ref = buf.at[r, c, parts[way]]
            copy = remote(ref, ref, send.at[r, way], recv.at[r, way], (east, west)[way % 2])
            return only(copy, r, way, x, early)

        def got(r, way):
            c = (col(COLS - 1), col(1), col(COLS - 1), col(1), col(2), col(2))[way]
            ref = buf.at[r, c, parts[way]]
            copy = remote(ref, ref, send.at[r, way], recv.at[r, way], (east, west)[way % 2])
            return only(copy, r, way, col((COLS - 1, 1)[way % 2]), early)

        return sent, got

    kv_sent, kv_got = ring(kv, kvx_send, kvx_recv, True)
    q_sent, q_got = ring(qt, qx_send, qx_recv, False)
    g_sent, g_got = ring(gat, gx_send, gx_recv, False)

    def pass_on(ring_sent, ring_got, r):
        ring_got(r, 0).wait_recv()
        ring_sent(r, 4).start()
        ring_got(r, 1).wait_recv()
        ring_got(r, 3).wait_recv()
        ring_sent(r, 5).start()
        ring_got(r, 2).wait_recv()

    def landed(ring_got, r):
        ring_got(r, 4).wait_recv()
        ring_got(r, 5).wait_recv()

    chunk = rows // CHUNKS

    def kv_north(r, part):
        piece = pl.ds(part * chunk, chunk)
        return remote(
            kv.at[r, x, piece], kv.at[r + 1, x, piece], kvy_send.at[r, part], kvy_recv.at[r, part], up(1)
        )

    def q_south(r):
        return remote(qt.at[r, x], qt.at[r + 1, x], qy_send.at[r], qy_recv.at[r], up(-1))

    def g_south(r):
        return remote(
            gat.at[(r - 1) // 2 * 2, x], gat.at[r, x], gy_send.at[r - 1], gy_recv.at[r - 1], up(-2 + r % 2)
        )

    grads = remote(gr_in, grx, g_sem.at[0], g_sem.at[1], partner)

    acc = [jnp.zeros((2 * HALF, rows), F32)]
    dq = [jnp.zeros((2 * HALF, rows), F32)]
    dk = [jnp.zeros((rows, HALF), F32)]
    dv = [jnp.zeros((rows, HALF), F32)]

    def tile(r, j):
        return 0 if r == 0 else (r - 1) * COLS + j + 1

    def behind(r, j):
        c = col(j)
        return (r, c) if r < REACH or j == 0 else (jnp.where(c < x, 0, REACH), c)

    def ahead(r, j):
        c = col(j)
        return (r, c) if r < REACH or j == 0 else (jnp.where(c > x, 0, REACH), c)

    def gated(h, live):
        th = jnp.tanh(h)
        u = h * th
        weights = jnp.where(live, h + u, 0.0).astype(BF16)
        return weights, jnp.where(live, (1.0 + th) * (1.0 + (h - u)), 0.0)

    def forward(r, j):
        rr, c = behind(r, j)
        t = tile(r, j)
        block = kv[rr, c]
        h = jnp.dot(block, qz, preferred_element_type=F32)
        base = ((y - rr) * COLS + c) * rows
        live = key_row >= start - base
        if r == 0:
            live = live & (key_row <= offset)
        weights, factor = gated(h, live)
        pt[t] = weights
        gf[t] = factor
        block_t = block.T
        kvt[t] = block_t
        acc[0] = acc[0] + jnp.dot(block_t, weights, preferred_element_type=F32)

    def key_side(r, j):
        rr, c = ahead(r, j)
        t = tile(r, j) - 1
        h = jnp.dot(keys_small, qt[rr, c], preferred_element_type=F32)
        live = key_row >= first_of(((y + rr) * COLS + c) * rows + offset) - s * rows
        pk[t], gk[t] = gated(h, live)

    def into_keys(ds, weights, queries, grad):
        nt = (((1,), (1,)), ((), ()))
        dk[0] = dk[0] + lax.dot_general(ds, queries, nt, preferred_element_type=F32)
        dv[0] = dv[0] + lax.dot_general(weights, grad, nt, preferred_element_type=F32)

    def spread(r):
        for half in range(2):
            for part in range(half * CHUNKS // 2, (half + 1) * CHUNKS // 2):
                if r > 0:
                    kv_north(r - 1, part).wait_recv()
                if r < REACH:
                    kv_north(r, part).start()
            kv_sent(r, 2 * half).start()
            kv_sent(r, 2 * half + 1).start()

    spread(0)
    loads[2].wait()
    grads.start()
    keys = qk[:, HALF:]
    values = vu[:, :HALF]
    qk_t = qk.astype(F32).T
    no_rows = jnp.zeros((HALF, rows), BF16)
    qz = jnp.concatenate([no_rows, (qk_t[:HALF] * (0.5 * HALF ** -0.5)).astype(BF16)], axis=0)
    qt[0, x] = qk_t[:HALF].astype(BF16)
    keys_small = (keys.astype(F32) * (0.5 * HALF ** -0.5)).astype(BF16)
    gate_in = vu.astype(F32).T[HALF:]
    gain = jnp.broadcast_to(gain_ref[...], (2 * HALF, HALF)).T[:, :1]
    ends = [len_ref[0, 0]]
    for user in range(1, len_ref.shape[1]):
        ends.append(ends[-1] + len_ref[0, user])
    offset = lax.broadcasted_iota(jnp.int32, (1, rows), 1)

    def first_of(position):
        start = jnp.zeros((1, rows), jnp.int32)
        for end in ends:
            start = jnp.where(position >= end, end, start)
        return start

    start = first_of(s * rows + offset)
    key_row = lax.broadcasted_iota(jnp.int32, (rows, rows), 0)

    q_south(0).start()
    forward(0, 0)
    for r in range(1, REACH + 1):
        spread(r)
        forward(r, 0)
        pass_on(kv_sent, kv_got, r - 1)
        if r >= 2:
            forward(r - 1, 1)
            forward(r - 1, 3)
            landed(kv_got, r - 2)
        if r >= 3:
            forward(r - 2, 2)
        q_south(r - 1).wait_recv()
        if r < REACH:
            q_south(r).start()
        if r < words:
            hear(r - 1)
            say(r)
    pass_on(kv_sent, kv_got, REACH)
    for r in range(REACH + 1):
        for way in range(4):
            q_sent(r, way).start()
    landed(kv_got, REACH - 1)
    forward(REACH - 1, 2)
    forward(REACH, 1)
    forward(REACH, 3)
    grads.wait()
    scaled = grx[...].astype(F32) * gain
    grad_norm = scaled * gate_in
    landed(kv_got, REACH)
    forward(REACH, 2)

    attended = acc[0][:HALF] * (1.0 / 256.0)
    sums = jnp.concatenate(
        [
            jnp.sum(value, axis=0, keepdims=True)
            for value in (attended, attended * attended, grad_norm, grad_norm * attended)
        ],
        axis=0,
    )
    stat[z] = jnp.concatenate([sums[:, : rows // 2], sums[:, rows // 2 :]], axis=0)

    def z_copy(k):
        return remote(
            stat.at[z], stat.at[z], z_send.at[k], z_recv.at[k], {"head": (z + k) % heads}
        )

    def z_start(k, carry):
        z_copy(k).start()
        return carry

    def z_wait(k, carry):
        z_copy(k).wait()
        return carry

    for i in range(min(words, REACH + 1) - 1, words):
        hear(i)
        if i + 1 < words:
            say(i + 1)
    lax.fori_loop(1, heads, z_start, 0)
    for r in range(REACH + 1):
        pass_on(q_sent, q_got, r)
    lax.fori_loop(1, heads, z_wait, 0)
    total = stat[0]
    for k in range(1, heads):
        total = total + stat[k]
    total = jnp.concatenate([total[:4], total[4:]], axis=1) * (1.0 / (HALF * heads))
    mean = total[0:1]
    rsigma = 1.0 / jnp.sqrt(jnp.maximum(total[1:2] - mean * mean, 0.0) + 1e-05)
    one = total[2:3]
    two = (total[3:4] - mean * one) * rsigma
    normed = (attended - mean) * rsigma
    grad_attn = ((grad_norm - one - normed * two) * rsigma).astype(BF16)
    gat[0, x] = grad_attn

    g_south(2).start()
    g_south(1).start()
    for way in range(4):
        g_sent(0, way).start()
    gate = scaled * normed
    gaz = jnp.concatenate([grad_attn, no_rows], axis=0)

    def query_side(r, j):
        rr, c = behind(r, j)
        t = tile(r, j)
        d_weights = jnp.dot(kv[rr, c], gaz, preferred_element_type=F32)
        ds = (d_weights * gf[t]).astype(BF16)
        dq[0] = dq[0] + jnp.dot(kvt[t], ds, preferred_element_type=F32)
        if r == 0:
            into_keys(ds, pt[0], qt[0, x], grad_attn)

    def key_grads(r, j):
        rr, c = ahead(r, j)
        t = tile(r, j) - 1
        grad = gat[rr, c]
        ds = (jnp.dot(values, grad, preferred_element_type=F32) * gk[t]).astype(BF16)
        into_keys(ds, pk[t], qt[rr, c], grad)

    def g_spread(r):
        g_south(r).wait_recv()
        if r == 2:
            g_south(4).start()
            g_south(3).start()
        for way in range(4):
            g_sent(r, way).start()

    for r in range(REACH + 1):
        landed(q_got, r)
    query_side(0, 0)
    for r in (1, 2):
        for j in range(COLS):
            query_side(r, j)
    g_spread(2)
    g_spread(1)
    pass_on(g_sent, g_got, 0)
    for r in (3, 4):
        for j in range(COLS):
            query_side(r, j)
    for r in (1, 2):
        for j in range(COLS):
            key_side(r, j)
    pass_on(g_sent, g_got, 2)
    pass_on(g_sent, g_got, 1)
    for r in (3, 4):
        for j in range(COLS):
            key_side(r, j)
    g_spread(3)
    g_spread(4)
    for r in (1, 2):
        for j in (0, 1, 3):
            key_grads(r, j)
    for r in (0, 2, 1):
        landed(g_got, r)
    key_grads(2, 2)
    key_grads(1, 2)
    pass_on(g_sent, g_got, 3)
    pass_on(g_sent, g_got, 4)
    for r in (3, 4):
        for j in (0, 1, 3):
            key_grads(r, j)
    packed = jnp.concatenate([dq[0][HALF:] * (1.0 / 4096.0), gate], axis=0).T
    landed(g_got, 3)
    key_grads(3, 2)
    landed(g_got, 4)
    key_grads(4, 2)
    oqk_ref[...] = jnp.concatenate([packed[:, :HALF], dk[0] * (1.0 / 4096.0)], axis=1).astype(BF16)
    ovu_ref[...] = jnp.concatenate([dv[0] * (1.0 / 256.0), packed[:, HALF:]], axis=1).astype(BF16)

    for r in range(REACH):
        for part in range(CHUNKS):
            kv_north(r, part).wait_send()
        q_south(r).wait_send()
        g_south(r + 1).wait_send()
    for r in range(REACH + 1):
        for way in range(6):
            kv_sent(r, way).wait_send()
            q_sent(r, way).wait_send()
            g_sent(r, way).wait_send()


def body(qk_rows, vu_rows, grad_next, layer_gain, user_lengths):
    rows, wide = qk_rows.shape[1], qk_rows.shape[3]
    heads = lax.axis_size("head")
    tiles = REACH * COLS + 1
    vmem = pl.BlockSpec(memory_space=pltpu.VMEM)
    hbm = pl.BlockSpec(memory_space=pltpu.HBM)
    dma = pltpu.SemaphoreType.DMA
    out = jax.ShapeDtypeStruct((rows, wide), BF16)
    grad_qk, grad_vu = pl.pallas_call(
        kernel,
        out_shape=(out, out),
        in_specs=[hbm, hbm, hbm, vmem, pl.BlockSpec(memory_space=pltpu.SMEM)],
        out_specs=(vmem, vmem),
        scratch_shapes=[
            pltpu.VMEM((REACH + 1, COLS, rows, wide), BF16),
            pltpu.VMEM((tiles, wide, rows), BF16),
            pltpu.VMEM((tiles, rows, rows), BF16),
            pltpu.VMEM((tiles, rows, rows), F32),
            pltpu.VMEM((tiles - 1, rows, rows), BF16),
            pltpu.VMEM((tiles - 1, rows, rows), F32),
            pltpu.VMEM((REACH + 1, COLS, wide // 2, rows), BF16),
            pltpu.VMEM((REACH + 1, COLS, wide // 2, rows), BF16),
            pltpu.VMEM((heads, 8, rows // 2), F32),
            pltpu.VMEM((wide // 2, rows), BF16),
            pltpu.VMEM((rows, wide), BF16),
            pltpu.VMEM((rows, wide), BF16),
            pltpu.VMEM((wide // 2, rows), BF16),
            dma((3,)),
            pltpu.SemaphoreType.REGULAR((2, heads // 2 - 1)),
            dma((2,)),
            dma((REACH, CHUNKS)),
            dma((REACH, CHUNKS)),
            dma((REACH + 1, 6)),
            dma((REACH + 1, 6)),
            dma((REACH,)),
            dma((REACH,)),
            dma((REACH + 1, 6)),
            dma((REACH + 1, 6)),
            dma((REACH,)),
            dma((REACH,)),
            dma((REACH + 1, 6)),
            dma((REACH + 1, 6)),
            dma((heads,)),
            dma((heads,)),
        ],
        compiler_params=pltpu.CompilerParams(
            collective_id=0, has_side_effects=True, vmem_limit_bytes=VMEM_BYTES
        ),
        name="attention_backward",
    )(
        qk_rows.reshape(rows, wide),
        vu_rows.reshape(rows, wide),
        grad_next.reshape(rows, wide // 2).T,
        layer_gain,
        user_lengths,
    )
    return grad_qk.reshape(1, rows, 1, wide), grad_vu.reshape(1, rows, 1, wide)


def solution(mesh):
    split = P("pipe", "seq", "head", None)
    return jax.shard_map(
        body,
        mesh=mesh,
        in_specs=(split, split, split, P("head", None), P("pipe", None)),
        out_specs=(split, split),
        check_vma=False,
    )
```

```python
import jax
import jax.numpy as jnp
from jax import lax
from jax.experimental import pallas as pl
from jax.experimental.pallas import tpu as pltpu
from jax.sharding import PartitionSpec as P

MESH = pl.DeviceIdType.MESH
F32 = jnp.float32
BF16 = jnp.bfloat16
COLS = 4
REACH = 4
HALF = 64
CHUNKS = 4
VMEM_BYTES = 67043328


class Guarded:
    def __init__(self, copy, when):
        self.copy, self.when = copy, when

    def start(self):
        pl.when(self.when)(self.copy.start)

    def wait_send(self):
        pl.when(self.when)(self.copy.wait_send)

    def wait_recv(self):
        pl.when(self.when)(self.copy.wait_recv)


def only(copy, r, way, at, early):
    if 0 < r < REACH:
        return copy
    if (r == 0) == early:
        when = (at <= 2, at == 0, at <= 2, at <= 1, (at == 1) | (at == 2), (at == 3) | (at == 0))[way]
    else:
        when = (at >= 2, at >= 1, at == 3, at >= 1, (at == 3) | (at == 0), (at == 1) | (at == 2))[way]
    return Guarded(copy, when)


def kernel(
    qk_ref, vu_ref, gr_ref, gain_ref, len_ref,
    oqk_ref, ovu_ref,
    kv, kvt, pt, gf, pk, gk, qt, gat, stat, grx,
    qk_in, vu_in, gr_in, in_sem, word, g_sem, kvy_send, kvy_recv, kvx_send, kvx_recv, qy_send, qy_recv, qx_send, qx_recv,
    gy_send, gy_recv, gx_send, gx_recv, z_send, z_recv,
):
    rows = qk_ref.shape[0]
    seqs = lax.axis_size("seq")
    heads = lax.axis_size("head")
    s, z, core = lax.axis_index("seq"), lax.axis_index("head"), lax.axis_index("pipe")
    x, y = s % COLS, s // COLS
    tall = seqs // COLS

    def col(j):
        return (x + j) % COLS

    def up(by):
        return {"seq": ((y + tall + by) % tall) * COLS + x}

    east = {"seq": y * COLS + col(1)}
    west = {"seq": y * COLS + col(COLS - 1)}
    partner = {"pipe": 1 - core}

    def remote(src, dst, send, recv, to):
        return pltpu.make_async_remote_copy(
            src_ref=src, dst_ref=dst, send_sem=send, recv_sem=recv, device_id=to, device_id_type=MESH
        )

    barrier = pltpu.get_barrier_semaphore()
    above, below = {"head": (z + 1) % heads}, {"head": (z + heads - 1) % heads}
    near = (east, west, up(1), up(-1), up(2), up(-2), partner, above, below)
    for to in near:
        pl.semaphore_signal(barrier, inc=1, device_id=to, device_id_type=MESH)

    loads = [
        pltpu.make_async_copy(src, dst, in_sem.at[i])
        for i, (src, dst) in enumerate(((qk_ref, qk_in), (vu_ref, vu_in), (gr_ref, gr_in)))
    ]
    for load in loads:
        load.start()
    loads[0].wait()
    loads[1].wait()
    qk = qk_in[...]
    vu = vu_in[...]
    lane = lax.broadcasted_iota(jnp.int32, (rows, 2 * HALF), 1)
    kv[0, x] = jnp.where(lane < HALF, vu, qk)
    pl.semaphore_wait(barrier, len(near))

    def say(i):
        pl.semaphore_signal(word.at[0, i], inc=1, device_id=above, device_id_type=MESH)
        pl.semaphore_signal(word.at[1, i], inc=1, device_id=below, device_id_type=MESH)

    def hear(i):
        pl.semaphore_wait(word.at[0, i], 1)
        pl.semaphore_wait(word.at[1, i], 1)

    words = heads // 2 - 1
    say(0)

    def ring(buf, send, recv, early):
        half = buf.shape[2] // 2
        low, high = pl.ds(0, half), pl.ds(half, half)
        parts = (low, low, high, high, low, high)

        def sent(r, way):
            c = (x, x, x, x, col(COLS - 1), col(1))[way]
            ref = buf.at[r, c, parts[way]]
            copy = remote(ref, ref, send.at[r, way], recv.at[r, way], (east, west)[way % 2])
            return only(copy, r, way, x, early)

        def got(r, way):
            c = (col(COLS - 1), col(1), col(COLS - 1), col(1), col(2), col(2))[way]
            ref = buf.at[r, c, parts[way]]
            copy = remote(ref, ref, send.at[r, way], recv.at[r, way], (east, west)[way % 2])
            return only(copy, r, way, col((COLS - 1, 1)[way % 2]), early)

        return sent, got

    kv_sent, kv_got = ring(kv, kvx_send, kvx_recv, True)
    q_sent, q_got = ring(qt, qx_send, qx_recv, False)
    g_sent, g_got = ring(gat, gx_send, gx_recv, False)

    def pass_on(ring_sent, ring_got, r):
        ring_got(r, 0).wait_recv()
        ring_sent(r, 4).start()
        ring_got(r, 3).wait_recv()
        ring_sent(r, 5).start()
        ring_got(r, 1).wait_recv()
        ring_got(r, 2).wait_recv()

    def landed(ring_got, r):
        ring_got(r, 4).wait_recv()
        ring_got(r, 5).wait_recv()

    chunk = rows // CHUNKS

    def kv_north(r, part):
        piece = pl.ds(part * chunk, chunk)
        return remote(
            kv.at[r, x, piece], kv.at[r + 1, x, piece], kvy_send.at[r, part], kvy_recv.at[r, part], up(1)
        )

    def q_south(r):
        return remote(qt.at[r, x], qt.at[r + 1, x], qy_send.at[r], qy_recv.at[r], up(-1))

    def g_south(r):
        return remote(
            gat.at[(r - 1) // 2 * 2, x], gat.at[r, x], gy_send.at[r - 1], gy_recv.at[r - 1], up(-2 + r % 2)
        )

    grads = remote(gr_in, grx, g_sem.at[0], g_sem.at[1], partner)

    acc = [jnp.zeros((2 * HALF, rows), F32)]
    dq = [jnp.zeros((2 * HALF, rows), F32)]
    dk = [jnp.zeros((rows, HALF), F32)]
    dv = [jnp.zeros((rows, HALF), F32)]

    def tile(r, j):
        return 0 if r == 0 else (r - 1) * COLS + j + 1

    def behind(r, j):
        c = col(j)
        return (r, c) if r < REACH or j == 0 else (jnp.where(c < x, 0, REACH), c)

    def ahead(r, j):
        c = col(j)
        return (r, c) if r < REACH or j == 0 else (jnp.where(c > x, 0, REACH), c)

    def gated(h, live):
        th = jnp.tanh(h)
        u = h * th
        weights = jnp.where(live, h + u, 0.0).astype(BF16)
        return weights, jnp.where(live, (1.0 + th) * (1.0 + (h - u)), 0.0)

    def forward(r, j):
        rr, c = behind(r, j)
        t = tile(r, j)
        block = kv[rr, c]
        h = jnp.dot(block, qz, preferred_element_type=F32)
        base = ((y - rr) * COLS + c) * rows
        live = key_row >= start - base
        if r == 0:
            live = live & (key_row <= offset)
        weights, factor = gated(h, live)
        pt[t] = weights
        gf[t] = factor
        block_t = block.T
        kvt[t] = block_t
        acc[0] = acc[0] + jnp.dot(block_t, weights, preferred_element_type=F32)

    def key_side(r, j):
        rr, c = ahead(r, j)
        t = tile(r, j) - 1
        h = jnp.dot(keys_small, qt[rr, c], preferred_element_type=F32)
        live = key_row >= first_of(((y + rr) * COLS + c) * rows + offset) - s * rows
        pk[t], gk[t] = gated(h, live)

    def into_keys(ds, weights, queries, grad):
        nt = (((1,), (1,)), ((), ()))
        dk[0] = dk[0] + lax.dot_general(ds, queries, nt, preferred_element_type=F32)
        dv[0] = dv[0] + lax.dot_general(weights, grad, nt, preferred_element_type=F32)

    def spread(r):
        for half in range(2):
            for part in range(half * CHUNKS // 2, (half + 1) * CHUNKS // 2):
                if r > 0:
                    kv_north(r - 1, part).wait_recv()
                if r < REACH:
                    kv_north(r, part).start()
            kv_sent(r, 2 * half).start()
            kv_sent(r, 2 * half + 1).start()

    spread(0)
    loads[2].wait()
    grads.start()
    keys = qk[:, HALF:]
    values = vu[:, :HALF]
    qk_t = qk.astype(F32).T
    no_rows = jnp.zeros((HALF, rows), BF16)
    qz = jnp.concatenate([no_rows, (qk_t[:HALF] * (0.5 * HALF ** -0.5)).astype(BF16)], axis=0)
    qt[0, x] = qk_t[:HALF].astype(BF16)
    keys_small = (keys.astype(F32) * (0.5 * HALF ** -0.5)).astype(BF16)
    gate_in = vu.astype(F32).T[HALF:]
    gain = jnp.broadcast_to(gain_ref[...], (2 * HALF, HALF)).T[:, :1]
    ends = [len_ref[0, 0]]
    for user in range(1, len_ref.shape[1]):
        ends.append(ends[-1] + len_ref[0, user])
    offset = lax.broadcasted_iota(jnp.int32, (1, rows), 1)

    def first_of(position):
        start = jnp.zeros((1, rows), jnp.int32)
        for end in ends:
            start = jnp.where(position >= end, end, start)
        return start

    start = first_of(s * rows + offset)
    key_row = lax.broadcasted_iota(jnp.int32, (rows, rows), 0)

    q_south(0).start()
    forward(0, 0)
    for r in range(1, REACH + 1):
        spread(r)
        forward(r, 0)
        pass_on(kv_sent, kv_got, r - 1)
        if r >= 2:
            forward(r - 1, 1)
            forward(r - 1, 3)
            landed(kv_got, r - 2)
        if r >= 3:
            forward(r - 2, 2)
        q_south(r - 1).wait_recv()
        if r < REACH:
            q_south(r).start()
        if r < words:
            hear(r - 1)
            say(r)
    pass_on(kv_sent, kv_got, REACH)
    for r in range(REACH + 1):
        for way in range(4):
            q_sent(r, way).start()
    landed(kv_got, REACH - 1)
    forward(REACH - 1, 2)
    forward(REACH, 1)
    forward(REACH, 3)
    grads.wait()
    scaled = grx[...].astype(F32) * gain
    grad_norm = scaled * gate_in
    landed(kv_got, REACH)
    forward(REACH, 2)

    attended = acc[0][:HALF] * (1.0 / 256.0)
    sums = jnp.concatenate(
        [
            jnp.sum(value, axis=0, keepdims=True)
            for value in (attended, attended * attended, grad_norm, grad_norm * attended)
        ],
        axis=0,
    )
    stat[z] = jnp.concatenate([sums[:, : rows // 2], sums[:, rows // 2 :]], axis=0)

    def z_copy(k):
        return remote(
            stat.at[z], stat.at[z], z_send.at[k], z_recv.at[k], {"head": (z + k) % heads}
        )

    def z_start(k, carry):
        z_copy(k).start()
        return carry

    def z_wait(k, carry):
        z_copy(k).wait()
        return carry

    for i in range(min(words, REACH + 1) - 1, words):
        hear(i)
        if i + 1 < words:
            say(i + 1)
    lax.fori_loop(1, heads, z_start, 0)
    for r in range(REACH + 1):
        pass_on(q_sent, q_got, r)
    lax.fori_loop(1, heads, z_wait, 0)
    total = stat[0]
    for k in range(1, heads):
        total = total + stat[k]
    total = jnp.concatenate([total[:4], total[4:]], axis=1) * (1.0 / (HALF * heads))
    mean = total[0:1]
    rsigma = 1.0 / jnp.sqrt(jnp.maximum(total[1:2] - mean * mean, 0.0) + 1e-05)
    one = total[2:3]
    two = (total[3:4] - mean * one) * rsigma
    normed = (attended - mean) * rsigma
    grad_attn = ((grad_norm - one - normed * two) * rsigma).astype(BF16)
    gat[0, x] = grad_attn

    g_south(2).start()
    g_south(1).start()
    for way in (0, 3, 2, 1):
        g_sent(0, way).start()
    gate = scaled * normed
    gaz = jnp.concatenate([grad_attn, no_rows], axis=0)

    def query_side(r, j):
        rr, c = behind(r, j)
        t = tile(r, j)
        d_weights = jnp.dot(kv[rr, c], gaz, preferred_element_type=F32)
        ds = (d_weights * gf[t]).astype(BF16)
        dq[0] = dq[0] + jnp.dot(kvt[t], ds, preferred_element_type=F32)
        if r == 0:
            into_keys(ds, pt[0], qt[0, x], grad_attn)

    def key_grads(r, j):
        rr, c = ahead(r, j)
        t = tile(r, j) - 1
        grad = gat[rr, c]
        ds = (jnp.dot(values, grad, preferred_element_type=F32) * gk[t]).astype(BF16)
        into_keys(ds, pk[t], qt[rr, c], grad)

    def g_spread(r):
        g_south(r).wait_recv()
        if r == 2:
            g_south(4).start()
            g_south(3).start()
        for way in (0, 3, 2, 1):
            g_sent(r, way).start()

    for r in range(REACH + 1):
        landed(q_got, r)
    query_side(0, 0)
    for r in (1, 2):
        for j in range(COLS):
            query_side(r, j)
    g_spread(2)
    g_spread(1)
    pass_on(g_sent, g_got, 0)
    for r in (3, 4):
        for j in range(COLS):
            query_side(r, j)
    for r in (1, 2):
        for j in range(COLS):
            key_side(r, j)
    pass_on(g_sent, g_got, 2)
    pass_on(g_sent, g_got, 1)
    for r in (3, 4):
        for j in range(COLS):
            key_side(r, j)
    g_spread(3)
    g_spread(4)
    for r in (1, 2):
        for j in (0, 1, 3):
            key_grads(r, j)
    for r in (0, 2, 1):
        landed(g_got, r)
    key_grads(2, 2)
    key_grads(1, 2)
    pass_on(g_sent, g_got, 3)
    pass_on(g_sent, g_got, 4)
    for r in (3, 4):
        for j in (0, 1, 3):
            key_grads(r, j)
    packed = jnp.concatenate([dq[0][HALF:] * (1.0 / 4096.0), gate], axis=0).T
    landed(g_got, 3)
    key_grads(3, 2)
    landed(g_got, 4)
    key_grads(4, 2)
    oqk_ref[...] = jnp.concatenate([packed[:, :HALF], dk[0] * (1.0 / 4096.0)], axis=1).astype(BF16)
    ovu_ref[...] = jnp.concatenate([dv[0] * (1.0 / 256.0), packed[:, HALF:]], axis=1).astype(BF16)

    for r in range(REACH):
        for part in range(CHUNKS):
            kv_north(r, part).wait_send()
        q_south(r).wait_send()
        g_south(r + 1).wait_send()
    for r in range(REACH + 1):
        for way in range(6):
            kv_sent(r, way).wait_send()
            q_sent(r, way).wait_send()
            g_sent(r, way).wait_send()


def body(qk_rows, vu_rows, grad_next, layer_gain, user_lengths):
    rows, wide = qk_rows.shape[1], qk_rows.shape[3]
    heads = lax.axis_size("head")
    tiles = REACH * COLS + 1
    vmem = pl.BlockSpec(memory_space=pltpu.VMEM)
    hbm = pl.BlockSpec(memory_space=pltpu.HBM)
    dma = pltpu.SemaphoreType.DMA
    out = jax.ShapeDtypeStruct((rows, wide), BF16)
    grad_qk, grad_vu = pl.pallas_call(
        kernel,
        out_shape=(out, out),
        in_specs=[hbm, hbm, hbm, vmem, pl.BlockSpec(memory_space=pltpu.SMEM)],
        out_specs=(vmem, vmem),
        scratch_shapes=[
            pltpu.VMEM((REACH + 1, COLS, rows, wide), BF16),
            pltpu.VMEM((tiles, wide, rows), BF16),
            pltpu.VMEM((tiles, rows, rows), BF16),
            pltpu.VMEM((tiles, rows, rows), F32),
            pltpu.VMEM((tiles - 1, rows, rows), BF16),
            pltpu.VMEM((tiles - 1, rows, rows), F32),
            pltpu.VMEM((REACH + 1, COLS, wide // 2, rows), BF16),
            pltpu.VMEM((REACH + 1, COLS, wide // 2, rows), BF16),
            pltpu.VMEM((heads, 8, rows // 2), F32),
            pltpu.VMEM((wide // 2, rows), BF16),
            pltpu.VMEM((rows, wide), BF16),
            pltpu.VMEM((rows, wide), BF16),
            pltpu.VMEM((wide // 2, rows), BF16),
            dma((3,)),
            pltpu.SemaphoreType.REGULAR((2, heads // 2 - 1)),
            dma((2,)),
            dma((REACH, CHUNKS)),
            dma((REACH, CHUNKS)),
            dma((REACH + 1, 6)),
            dma((REACH + 1, 6)),
            dma((REACH,)),
            dma((REACH,)),
            dma((REACH + 1, 6)),
            dma((REACH + 1, 6)),
            dma((REACH,)),
            dma((REACH,)),
            dma((REACH + 1, 6)),
            dma((REACH + 1, 6)),
            dma((heads,)),
            dma((heads,)),
        ],
        compiler_params=pltpu.CompilerParams(
            collective_id=0, has_side_effects=True, vmem_limit_bytes=VMEM_BYTES
        ),
        name="attention_backward",
    )(
        qk_rows.reshape(rows, wide),
        vu_rows.reshape(rows, wide),
        grad_next.reshape(rows, wide // 2).T,
        layer_gain,
        user_lengths,
    )
    return grad_qk.reshape(1, rows, 1, wide), grad_vu.reshape(1, rows, 1, wide)


def solution(mesh):
    split = P("pipe", "seq", "head", None)
    return jax.shard_map(
        body,
        mesh=mesh,
        in_specs=(split, split, split, P("head", None), P("pipe", None)),
        out_specs=(split, split),
        check_vma=False,
    )
```
